256 devices in a mesh: gx: 8 (over z), gy: 16 (over x, y_hi, core), layer: 2 (over y_lo).
Axes of the slice: x: 4, y: 4 (y_hi: 2, y_lo: 2; y = y_hi * 2 + y_lo), z: 8, core: 2. Of those that a mesh axis runs over, the one named last changes fastest.
Arguments:
- atom_feats: bfloat16 [16384, 128], P(('gx', 'gy', 'layer')), may hold values from -6 to 6
- bond_embed: bfloat16 [589824, 128], P(('gx', 'gy', 'layer')), may hold values from -6 to 6
- pair_dist: float32 [1179648], P(('gx', 'gy', 'layer')), may hold values from 1.4 to 6.9
- neighbours: int32 [1179648], P(('gx', 'gy', 'layer')), may hold values from 0 to 1151, as said below
- slot_kind: int32 [1179648], P(('gx', 'gy', 'layer')), may hold values from 0 to 2
- own_rows: int32 [589824], P(('gx', 'gy', 'layer')), may hold values from 0 to 4607, as said below
- send_pos: int32 [589824], P(('gx', 'gy', 'layer')), may hold values from 0 to 2303, as said below
- recv_pos: int32 [1179648], P(('gx', 'gy', 'layer')), may hold values from 0 to 2303, as said below
- w_left: bfloat16 [3, 128, 128], replicated, may hold values from -0.5 to 0.5
- w_right: bfloat16 [3, 128, 128], replicated, may hold values from -0.5 to 0.5
- w_edge_in: bfloat16 [3, 128, 128], replicated, may hold values from -0.5 to 0.5
- w_edge_out: bfloat16 [3, 128, 128], replicated, may hold values from -0.5 to 0.5
- w_msg: bfloat16 [2, 128, 128], replicated, may hold values from -0.5 to 0.5
- w_upd: bfloat16 [2, 128, 128], replicated, may hold values from -0.5 to 0.5
- node_gain: float32 [2, 128], replicated, may hold values from 0.1 to 1.9
- w_block: bfloat16 [128, 169], replicated, may hold values from -0.5 to 0.5
Outputs:
- blocks: bfloat16 [169, 1179648], P(None, ('gx', 'gy', 'layer'))
The draws below stay inside these ranges and needn't reach their ends.
Inputs may be any that keep to these rules, and one draw needn't show every extreme that they name: `neighbours`: slots pair up: a slot of kind 1 or 2 and the slot of its partner atom that points back form one pair, one of kind 1 and the other of kind 2, with equal distance; empty slots pair with empty slots. Each atom has 4 slots towards each of the 18 offsets, half of them owned. `own_rows`: each domain's rows list its 2304 owned slots once each; the valid ones (kind 1) come first, at most 2112 of them, and some domain has exactly 2112. `send_pos`: within a domain every value occurs once; value // 128 is the offset of the partner's domain. `recv_pos`: for slots of kind 2: value // 128 is the reverse of the offset of the partner's domain.
All inputs are finite; a program needn't handle non-finite values.
Results may differ from the reference program's by a relative error of at most 0.019.
Values may be sent and summed in bfloat16 or wider, within the bound.
A program may use at most 64 MiB of HBM per device.

```python
import jax
import jax.numpy as jnp
from jax import lax

C = 128
ORB = 13
BLOCK = 169
ATOM_DEV = 64
GROUPS = 4
NEIGH = 72
LAYERS = 3
OWN = 2304
VCAP = 2112
CAP = 128
ATOMS = 16384
OWNED = 589824
N_GX = 8
N_GY = 16
N_LAYER = 2


def partner_device_drawn(device, offset):
    sheet_step = offset // 9
    step_x = offset % 9 // 3 - 1
    step_y = offset % 3 - 1
    grid_x = device // (N_GY * N_LAYER)
    grid_y = device // N_LAYER % N_GY
    sheet_now = device % N_LAYER
    return ((grid_x + step_x) % N_GX * (N_GY * N_LAYER) + (grid_y + step_y) % N_GY * N_LAYER + (sheet_now + sheet_step) % N_LAYER).astype(jnp.int32)


def layout_tables(key):
    devices = N_GX * N_GY * N_LAYER
    half_groups = GROUPS // 2
    fanout = 18 * GROUPS
    capacity = half_groups * ATOM_DEV
    base_key = jax.random.fold_in(key, 4021)
    key_pairs, key_slots, key_order, key_count, key_pick, key_length = jax.random.split(base_key, 6)
    pair_base = jnp.broadcast_to(jnp.arange(ATOM_DEV, dtype=jnp.int32), (devices * 18 * half_groups, ATOM_DEV))
    forward = jax.random.permutation(key_pairs, pair_base, axis=1, independent=True).reshape(devices, 18, half_groups, ATOM_DEV)
    backward = jnp.argsort(forward, axis=-1).astype(jnp.int32)
    device_ids = jnp.arange(devices, dtype=jnp.int32)[:, None, None, None]
    offsets = jnp.arange(18, dtype=jnp.int32)[None, :, None, None]
    groups = jnp.arange(GROUPS, dtype=jnp.int32)[None, None, :, None]
    atom_ids = jnp.arange(ATOM_DEV, dtype=jnp.int32)[None, None, None, :]
    reverse = offsets // 9 * 9 + 8 - offsets % 9
    source = partner_device_drawn(device_ids, offsets)
    is_owner = groups < half_groups
    low_group = jnp.minimum(groups, half_groups - 1)
    high_group = jnp.maximum(groups - half_groups, 0)
    source_atom = backward[source, reverse, high_group, atom_ids]
    peer_atom = jnp.where(is_owner, forward[device_ids, offsets, low_group, atom_ids], source_atom)
    counts = jax.random.randint(key_count, (devices,), OWN * 78 // 100, VCAP + 1).astype(jnp.int32)
    counts = counts.at[jax.random.randint(key_pick, (), 0, devices)].set(VCAP)
    order_base = jnp.broadcast_to(jnp.arange(OWN, dtype=jnp.int32), (devices, OWN))
    ordering = jax.random.permutation(key_order, order_base, axis=1, independent=True).astype(jnp.int32)
    ranking = jnp.argsort(ordering, axis=1).astype(jnp.int32)
    owned_valid = (ranking < counts[:, None]).reshape(devices, 18, half_groups, ATOM_DEV)
    owned_code = jax.random.randint(key_length, (devices, 18, half_groups, ATOM_DEV), 0, 1048576)
    valid_full = jnp.where(is_owner, owned_valid[device_ids, offsets, low_group, atom_ids], owned_valid[source, reverse, high_group, source_atom])
    code_full = jnp.where(is_owner, owned_code[device_ids, offsets, low_group, atom_ids], owned_code[source, reverse, high_group, source_atom])
    slot_base = jnp.broadcast_to(jnp.arange(fanout, dtype=jnp.int32), (devices * ATOM_DEV, fanout))
    shuffle = jax.random.permutation(key_slots, slot_base, axis=1, independent=True).reshape(devices, ATOM_DEV, fanout).astype(jnp.int32)
    placing = jnp.argsort(shuffle, axis=-1).astype(jnp.int32)
    slot_offset = shuffle // GROUPS
    slot_group = shuffle % GROUPS
    device_index = jnp.arange(devices, dtype=jnp.int32)[:, None, None]
    atom_index = jnp.arange(ATOM_DEV, dtype=jnp.int32)[None, :, None]
    stored_peer = peer_atom[device_index, slot_offset, slot_group, atom_index]
    stored_valid = valid_full[device_index, slot_offset, slot_group, atom_index]
    stored_code = code_full[device_index, slot_offset, slot_group, atom_index]
    neighbour_ids = (slot_offset * ATOM_DEV + stored_peer).astype(jnp.int32)
    kinds = jnp.where(stored_valid, jnp.where(slot_group < half_groups, 1, 2), 0).astype(jnp.int32)
    stored_reverse = slot_offset // 9 * 9 + 8 - slot_offset % 9
    receive = jnp.where(slot_group >= half_groups, stored_reverse * capacity + (slot_group - half_groups) * ATOM_DEV + stored_peer, 0).astype(jnp.int32)
    own_offset = ordering // (half_groups * ATOM_DEV)
    own_group = ordering // ATOM_DEV % half_groups
    own_atom = ordering % ATOM_DEV
    device_column = jnp.arange(devices, dtype=jnp.int32)[:, None]
    rows_listed = (own_atom * fanout + placing[device_column, own_atom, own_offset * GROUPS + own_group]).astype(jnp.int32)
    sending = (own_offset * capacity + own_group * ATOM_DEV + own_atom).astype(jnp.int32)
    return (neighbour_ids.reshape(-1), kinds.reshape(-1), rows_listed.reshape(-1), sending.reshape(-1), receive.reshape(-1), stored_code.reshape(-1))


def draw_pair_dist(key, part):
    fraction = layout_tables(key)[5].astype(jnp.float32) / 1048576.0
    return 1.4 + 5.5 * fraction


def draw_neighbours(key, part):
    return layout_tables(key)[0]


def draw_slot_kind(key, part):
    return layout_tables(key)[1]


def draw_own_rows(key, part):
    return layout_tables(key)[2]


def draw_send_pos(key, part):
    return layout_tables(key)[3]


def draw_recv_pos(key, part):
    return layout_tables(key)[4]


def block_scale(own_key, dims, cuts, low, high):
    def one(axis_at, parts):
        steps = jax.random.uniform(jax.random.fold_in(jax.random.fold_in(own_key, 6), axis_at), (parts,), jnp.float32, low / len(cuts), high / len(cuts))
        return jnp.repeat(jnp.exp(steps), dims[axis_at] // parts).reshape((-1,) + (1,) * (len(dims) - axis_at - 1))

    loudness = one(*cuts[0])
    for cut in cuts[1:]:
        loudness = loudness * one(*cut)
    return loudness


def gaussian(stream_key, extent, scale, most, shards=(), held_as=jnp.bfloat16):
    loudness = block_scale(stream_key, extent, shards, -0.22, 0.18) if shards else 1.0
    entries = jax.random.normal(stream_key, extent, jnp.float32) * scale * loudness
    return jnp.minimum(jnp.maximum(entries, -most), most).astype(held_as)


def setup_inputs(seed: int = 0) -> dict:
    streams_of = jax.random.split(jax.random.key(seed), 17)
    atom_feats = gaussian(streams_of[0], (ATOMS, C), 1.0, 6.0, ((0, 256),))
    bond_embed = gaussian(streams_of[1], (OWNED, C), 1.0, 6.0, ((0, 256),))
    pair_dist = draw_pair_dist(jax.random.fold_in(streams_of[16], 71), 0)
    neighbours = draw_neighbours(jax.random.fold_in(streams_of[16], 71), 0)
    slot_kind = draw_slot_kind(jax.random.fold_in(streams_of[16], 71), 0)
    own_rows = draw_own_rows(jax.random.fold_in(streams_of[16], 71), 0)
    send_pos = draw_send_pos(jax.random.fold_in(streams_of[16], 71), 0)
    recv_pos = draw_recv_pos(jax.random.fold_in(streams_of[16], 71), 0)
    w_left = gaussian(streams_of[8], (LAYERS, C, C), C ** -0.5, 0.5)
    w_right = gaussian(streams_of[9], (LAYERS, C, C), C ** -0.5, 0.5)
    w_edge_in = gaussian(streams_of[10], (LAYERS, C, C), C ** -0.5, 0.5)
    w_edge_out = gaussian(streams_of[11], (LAYERS, C, C), C ** -0.5, 0.5)
    w_msg = gaussian(streams_of[12], (LAYERS - 1, C, C), C ** -0.5, 0.5)
    w_upd = gaussian(streams_of[13], (LAYERS - 1, C, C), C ** -0.5, 0.5)
    node_gain = jnp.clip(1.0 + 0.18 * jax.random.normal(streams_of[14], (LAYERS - 1, C), jnp.float32), 0.1, 1.9)
    w_block = gaussian(streams_of[15], (C, BLOCK), C ** -0.5, 0.5)
    return {"atom_feats": atom_feats, "bond_embed": bond_embed, "pair_dist": pair_dist, "neighbours": neighbours, "slot_kind": slot_kind, "own_rows": own_rows, "send_pos": send_pos, "recv_pos": recv_pos, "w_left": w_left, "w_right": w_right, "w_edge_in": w_edge_in, "w_edge_out": w_edge_out, "w_msg": w_msg, "w_upd": w_upd, "node_gain": node_gain, "w_block": w_block}


def partner_device(device, offset):
    sheet_step = offset // 9
    step_x = offset % 9 // 3 - 1
    step_y = offset % 3 - 1
    grid_x = device // (N_GY * N_LAYER)
    grid_y = device // N_LAYER % N_GY
    sheet_now = device % N_LAYER
    return ((grid_x + step_x) % N_GX * (N_GY * N_LAYER) + (grid_y + step_y) % N_GY * N_LAYER + (sheet_now + sheet_step) % N_LAYER).astype(jnp.int32)

def rms_norm(values):
    return values * lax.rsqrt(lax.optimization_barrier(jnp.mean(values * values, axis=-1, keepdims=True)) + 1e-06)

def cutoff(distance):
    scaled = distance / 7.0
    return (1.0 - scaled * scaled) ** 2

def reference(atom_feats, bond_embed, pair_dist, neighbours, slot_kind, own_rows, send_pos, recv_pos, w_left, w_right, w_edge_in, w_edge_out, w_msg, w_upd, node_gain, w_block):
    devices = N_GX * N_GY * N_LAYER
    slot_dev = ATOM_DEV * NEIGH
    channels = atom_feats.shape[1]
    slot_device = (jnp.arange(devices * slot_dev, dtype=jnp.int32) // slot_dev).astype(jnp.int32)
    peer_global = (partner_device(slot_device, neighbours // ATOM_DEV) * ATOM_DEV + neighbours % ATOM_DEV).astype(jnp.int32)
    row_device = (jnp.arange(devices * OWN, dtype=jnp.int32) // OWN).astype(jnp.int32)
    row_slot = (row_device * slot_dev + own_rows).astype(jnp.int32)
    row_atom = (row_slot // NEIGH).astype(jnp.int32)
    row_peer = peer_global[row_slot]
    envelope = cutoff(pair_dist) * (slot_kind > 0).astype(jnp.float32)
    hidden = atom_feats
    edge_state = bond_embed
    for layer_index in range(LAYERS):
        near_proj = jnp.dot(hidden, w_left[layer_index], preferred_element_type=jnp.float32).astype(jnp.bfloat16)
        far_proj = jnp.dot(hidden, w_right[layer_index], preferred_element_type=jnp.float32).astype(jnp.bfloat16)
        edge_in = w_edge_in[layer_index]
        edge_out = w_edge_out[layer_index]

        def edge_step(pieces):
            state_rows, atom_index, peer_index = pieces
            inner_proj = jnp.dot(state_rows, edge_in, preferred_element_type=jnp.float32)
            mixed_gate = jax.nn.silu(inner_proj * near_proj[atom_index].astype(jnp.float32) * far_proj[peer_index].astype(jnp.float32)).astype(jnp.bfloat16)
            renewed = state_rows.astype(jnp.float32) + jnp.dot(mixed_gate, edge_out, preferred_element_type=jnp.float32)
            return rms_norm(renewed).astype(jnp.bfloat16)
        new_state = lax.map(edge_step, (edge_state.reshape(devices, OWN, channels), row_atom.reshape(devices, OWN), row_peer.reshape(devices, OWN)))
        if layer_index + 1 < LAYERS:
            message = jnp.dot(hidden, w_msg[layer_index], preferred_element_type=jnp.float32).astype(jnp.bfloat16)

            def node_step(pieces):
                peer_ids, weights = pieces
                gathered = message[peer_ids].astype(jnp.float32) * weights[:, None]
                return (lax.optimization_barrier(jnp.sum(gathered.reshape(ATOM_DEV, NEIGH, channels), axis=1)) * 0.125).astype(jnp.bfloat16)
            summed = lax.map(node_step, (peer_global.reshape(devices, slot_dev), envelope.reshape(devices, slot_dev))).reshape(devices * ATOM_DEV, channels)
            updated = hidden.astype(jnp.float32) + jax.nn.silu(jnp.dot(summed, w_upd[layer_index], preferred_element_type=jnp.float32))
            hidden = (rms_norm(updated) * node_gain[layer_index].astype(jnp.float32)).astype(jnp.bfloat16)
        edge_state = new_state.reshape(devices * OWN, channels)
    swapped = w_block.reshape(channels, ORB, ORB).transpose(0, 2, 1).reshape(channels, ORB * ORB)
    device_rows = jnp.arange(devices, dtype=jnp.int32)[:, None]
    inverse_row = jnp.zeros((devices, 18 * CAP), jnp.int32).at[device_rows, send_pos.reshape(devices, OWN)].set(jnp.broadcast_to(jnp.arange(OWN, dtype=jnp.int32), (devices, OWN)))

    def block_step(device_index):
        start = (device_index * slot_dev).astype(jnp.int32)
        kind_here = lax.dynamic_slice_in_dim(slot_kind, start, slot_dev)
        nbr_here = lax.dynamic_slice_in_dim(neighbours, start, slot_dev)
        recv_here = lax.dynamic_slice_in_dim(recv_pos, start, slot_dev)
        row_start = (device_index * OWN).astype(jnp.int32)
        state_rows = lax.dynamic_slice_in_dim(edge_state, row_start, OWN)
        rows_here = lax.dynamic_slice_in_dim(own_rows, row_start, OWN)
        direct = lax.dot_general(w_block, state_rows, (((0,), (1,)), ((), ())), preferred_element_type=jnp.float32)
        own_part = jnp.zeros((ORB * ORB, slot_dev), jnp.float32).at[:, rows_here].set(direct)
        sender = partner_device(device_index, nbr_here // ATOM_DEV)
        sender_row = inverse_row[sender, recv_here]
        far_rows = edge_state[(sender * OWN + sender_row).astype(jnp.int32)]
        mirror = lax.dot_general(swapped, far_rows, (((0,), (1,)), ((), ())), preferred_element_type=jnp.float32)
        chosen = jnp.where(kind_here == 1, own_part, jnp.where(kind_here == 2, mirror, jnp.zeros_like(mirror)))
        return chosen.astype(jnp.bfloat16)
    per_device = lax.map(block_step, jnp.arange(devices, dtype=jnp.int32))
    return jnp.moveaxis(per_device, 0, 1).reshape(ORB * ORB, devices * slot_dev)
```

```python
import jax
import jax.numpy as jnp
from jax import lax
from jax.experimental import pallas as pl
from jax.experimental.pallas import tpu as pltpu
from jax.sharding import PartitionSpec as P

ORB = 13
LAYERS = 3
OFFSETS = 18
SELF = 4
ATOMS = 64
NEIGH = 72
SLOTS = ATOMS * NEIGH
CAP = 128
LISTED = 2176
MESH = pl.DeviceIdType.MESH
BF = jnp.bfloat16
F32 = jnp.float32
NT = (((1,), (1,)), ((), ()))


def dot(a, b):
    return jnp.dot(a, b, preferred_element_type=F32)


def dot_nt(a, b):
    return lax.dot_general(a, b, NT, preferred_element_type=F32)


def silu(v):
    half = 0.5 * v
    return half + half * jnp.tanh(half)


def reverse_of(offset):
    return offset // 9 * 9 + 8 - offset % 9


def kernel(
    atom_ref,
    bond_ref,
    slot_ref,
    dist_ref,
    owned_ref,
    wl_ref,
    wr_ref,
    wi_ref,
    wo_ref,
    wm_ref,
    wu_ref,
    gain_ref,
    wb_ref,
    out_ref,
    ghost,
    hidden,
    bond_send,
    bond_recv,
    rows,
    pick_far,
    mix,
    tables,
    message,
    edge,
    last,
    wide,
    place,
    spread,
    blocks,
    send_sem,
    recv_sem,
):
    gx, gy, sheet = lax.axis_index("gx"), lax.axis_index("gy"), lax.axis_index("layer")
    n_gx, n_gy = lax.axis_size("gx"), lax.axis_size("gy")

    def partner(offset):
        step_x = offset % 9 // 3 - 1
        step_y = offset % 3 - 1
        return (
            (gx + step_x + n_gx) % n_gx,
            (gy + step_y + n_gy) % n_gy,
            (sheet + offset // 9) % 2,
        )

    others = [o for o in range(OFFSETS) if o != SELF]

    barrier = pltpu.get_barrier_semaphore()
    for o in others:
        pl.semaphore_signal(barrier, inc=1, device_id=partner(o), device_id_type=MESH)
    pl.semaphore_wait(barrier, len(others))

    def ghost_copy(layer, o):
        source = atom_ref if layer == 0 else hidden.at[layer - 1]
        return pltpu.make_async_remote_copy(
            src_ref=source,
            dst_ref=ghost.at[layer, reverse_of(o)],
            send_sem=send_sem.at[layer, o],
            recv_sem=recv_sem.at[layer, reverse_of(o)],
            device_id=partner(o),
            device_id_type=MESH,
        )

    def bond_copy(o):
        return pltpu.make_async_remote_copy(
            src_ref=bond_send.at[o],
            dst_ref=bond_recv.at[reverse_of(o)],
            send_sem=send_sem.at[3, o],
            recv_sem=recv_sem.at[3, reverse_of(o)],
            device_id=partner(o),
            device_id_type=MESH,
        )

    for o in others:
        ghost_copy(0, o).start()
    ghost[0, SELF] = atom_ref[...]

    slot = slot_ref[...]
    nbr, kind, place_in = slot & 2047, (slot >> 11) & 3, slot >> 13
    offset_of = nbr >> 6
    atom_of = ((nbr & 63) + 1).astype(F32)
    scaled = dist_ref[...] / 7.0
    falloff = 1.0 - scaled * scaled
    env = jnp.where(kind > 0, falloff * falloff, 0.0)
    own_key = jnp.where(kind == 1, offset_of, -1)
    far_key = jnp.where(kind == 2, offset_of, -1)
    recv_place = (place_in + 1).astype(F32)

    sub72 = lax.broadcasted_iota(jnp.int32, (NEIGH, 128), 0)
    sub = lax.broadcasted_iota(jnp.int32, (128, 128), 0)
    lane = lax.broadcasted_iota(jnp.int32, (128, 128), 1)

    send_place = jnp.zeros((NEIGH, 128), F32)
    for k in range(OFFSETS):
        owned = owned_ref[k : k + 1, :]
        at_slot = jnp.where(((owned >> 6) & 127) == sub72, 1.0, 0.0).astype(BF)
        value = (((owned >> 13) & 127) + 1).astype(F32)
        at_atom = jnp.where((owned & 63) == (sub & 63), value, 0.0).astype(BF)
        send_place = send_place + dot_nt(at_slot, at_atom)

    before = jnp.where(
        lax.broadcasted_iota(jnp.int32, (NEIGH, NEIGH), 0)
        > lax.broadcasted_iota(jnp.int32, (NEIGH, NEIGH), 1),
        1.0,
        0.0,
    ).astype(BF)
    rank_lane = (lax.broadcasted_iota(jnp.int32, (NEIGH, 128), 1) >> 6).astype(F32)

    def total(v):
        return jnp.sum(v, axis=0, keepdims=True)

    def tables_step(o, where_to):
        own = jnp.where(own_key == o, 1.0, 0.0)
        far = jnp.where(far_key == o, 1.0, 0.0)
        count = dot(before, jnp.concatenate([own, far], axis=1).astype(BF))
        own_rank, far_rank = count[:, :128], count[:, 128:]
        own_hit = jnp.where(own_rank == rank_lane, own, 0.0)
        far_hit = jnp.where(far_rank == rank_lane, far, 0.0)
        rows[0, pl.ds(o, 1), :] = total(own_hit * atom_of) - 1.0
        rows[1, pl.ds(o, 1), :] = total(far_hit * atom_of) - 1.0
        rows[2, pl.ds(o, 1), :] = total(own_hit * send_place) - 1.0
        rows[3, pl.ds(o, 1), :] = total(far_hit * recv_place) - 1.0
        rows[4, pl.ds(o, 1), :] = total(own_hit * env)
        rows[5, pl.ds(o, 1), :] = total(far_hit * env)
        base = (4 * o + 1).astype(F32)
        return where_to + own * (own_rank + base) + far * (far_rank + (base + 2.0))

    where_to = lax.fori_loop(0, OFFSETS, tables_step, jnp.zeros((NEIGH, 128), F32))

    subf = (sub & 63).astype(F32)
    for g in range(OFFSETS // 2):
        low = sub < 64

        def pair(kind_of_row):
            first = rows[kind_of_row, 2 * g : 2 * g + 1, :]
            second = rows[kind_of_row, 2 * g + 1 : 2 * g + 2, :]
            return jnp.where(low, first, second)

        weights = jnp.where(pair(0) == subf, pair(4), 0.0) + jnp.where(
            pair(1) == subf, pair(5), 0.0
        )
        mix[:, g * 128 : (g + 1) * 128] = weights.T.astype(BF)

    sub384 = lax.broadcasted_iota(jnp.int32, (384, 128), 0)

    def bond_step(step, carry):
        first = step * 384
        picked = [
            jnp.where((owned_ref[k : k + 1, :] >> 13) - first == sub384, 1.0, 0.0).astype(BF)
            for k in range(LISTED // 128)
        ]
        got = dot(jnp.concatenate(picked, axis=1), bond_ref[:LISTED, :]).astype(BF)
        for i in range(3):
            o = step * 3 + i
            bond_send[o] = got[i * 128 : (i + 1) * 128, :]

            @pl.when(o != SELF)
            def _():
                bond_copy(o).start()

        return carry

    lax.fori_loop(0, OFFSETS // 3, bond_step, 0)

    def wait_ghost(layer):
        for o in others:
            pltpu.make_async_remote_copy(
                src_ref=ghost.at[layer, o],
                dst_ref=ghost.at[layer, o],
                send_sem=send_sem.at[layer, o],
                recv_sem=recv_sem.at[layer, o],
                device_id=partner(o),
                device_id_type=MESH,
            ).wait_recv()

    def update_hidden(layer):
        ghosts = ghost[layer].reshape(OFFSETS * ATOMS, 128)
        message[...] = dot(ghosts, wm_ref[layer]).astype(BF)
        two = dot(mix[...], message[...])
        summed = ((two[:ATOMS] + two[ATOMS:]) * 0.125).astype(BF)
        updated = ghost[layer, SELF].astype(F32) + silu(dot(summed, wu_ref[layer]))
        mean = jnp.mean(updated * updated, axis=-1, keepdims=True)
        fresh = updated * lax.rsqrt(mean + 1e-06) * gain_ref[layer : layer + 1, :]
        hidden[layer] = fresh.astype(BF)
        for o in others:
            ghost_copy(layer + 1, o).start()
        ghost[layer + 1, SELF] = fresh.astype(BF)

    def project(layer):
        both = jnp.concatenate([wr_ref[layer], wl_ref[layer]], axis=1)

        def one(o, carry):
            got = dot(ghost[layer, o], both).astype(BF)
            tables[o, 0:64, 0:128] = got[:, :128]
            tables[o, 64:128, 128:256] = got[:, 128:]
            return carry

        lax.fori_loop(0, OFFSETS, one, 0)

    ones = jnp.full((128, 128), 1.0 / 128.0, BF)

    def edge_layer(layer, final):
        right = tables[SELF, 0:64, 0:128].astype(F32)
        left = tables[SELF, 64:128, 128:256].astype(F32)
        left2 = jnp.concatenate([left, left], axis=0)
        right2 = jnp.concatenate([right, right], axis=0)
        edge_in, edge_out = wi_ref[layer], wo_ref[layer]

        def one(o, carry):
            state = edge[o]
            reached = dot(pick_far[o], tables[o])
            product = jnp.concatenate(
                [reached[:, :128] * left2, reached[:, 128:] * right2], axis=0
            )
            gate = silu(dot(state, edge_in) * product).astype(BF)
            renewed = state.astype(F32) + dot(gate, edge_out)
            mean = jnp.mean(renewed * renewed, axis=-1, keepdims=True)
            fresh = renewed * lax.rsqrt(mean + 1e-06)
            if final:
                last[pl.ds(o * 256, 256), :] = fresh
            else:
                edge[o] = fresh.astype(BF)
            return carry

        lax.fori_loop(0, OFFSETS, one, 0)

    wait_ghost(0)
    update_hidden(0)

    tables[...] = jnp.zeros_like(tables)

    def far_step(o, carry):
        own_atom, far_atom = rows[0, pl.ds(o, 1), :], rows[1, pl.ds(o, 1), :]
        wanted = jnp.where(sub < 64, own_atom, far_atom)
        pick_far[o] = jnp.where(wanted == subf, 1.0, 0.0).T.astype(BF)
        return carry

    lax.fori_loop(0, OFFSETS, far_step, 0)
    project(0)

    subq = sub.astype(F32)

    def own_step(o, carry):
        wanted = rows[2, pl.ds(o, 1), :]
        picker = jnp.where(wanted == subq, 1.0, 0.0).T.astype(BF)
        edge[o, 0:128, :] = dot(picker, bond_send[o]).astype(BF)
        return carry

    lax.fori_loop(0, OFFSETS, own_step, 0)

    for n in range(ATOMS):
        spread[n * NEIGH : (n + 1) * NEIGH, :] = jnp.broadcast_to(
            where_to[:, n : n + 1], (NEIGH, 128)
        ) + jnp.where(
            jnp.broadcast_to(where_to[:, n : n + 1], (NEIGH, 128)) > 0.0, n * 72.0 - 1.0, -1.0
        )

    def place_step(i, carry):
        start = jnp.clip(i * 256 - 128, 0, SLOTS - 512)
        column = spread[pl.ds(pl.multiple_of(i * 256, 256), 256), :]
        for k in range(4):
            here = (lax.broadcasted_iota(jnp.int32, (256, 128), 1) + (start + k * 128)).astype(F32)
            place[i, :, k * 128 : (k + 1) * 128] = jnp.where(column == here, 1.0, 0.0).astype(BF)
        return carry

    lax.fori_loop(0, SLOTS // 256, place_step, 0)

    for o in others:
        pltpu.make_async_remote_copy(
            src_ref=bond_recv.at[o],
            dst_ref=bond_recv.at[o],
            send_sem=send_sem.at[3, o],
            recv_sem=recv_sem.at[3, o],
            device_id=partner(o),
            device_id_type=MESH,
        ).wait_recv()
    bond_recv[SELF] = bond_send[SELF]

    def recv_step(o, carry):
        wanted = rows[3, pl.ds(o, 1), :]
        picker = jnp.where(wanted == subq, 1.0, 0.0).T.astype(BF)
        edge[o, 128:256, :] = dot(picker, bond_recv[o]).astype(BF)
        return carry

    lax.fori_loop(0, OFFSETS, recv_step, 0)
    edge_layer(0, False)

    wait_ghost(1)
    update_hidden(1)
    project(1)
    edge_layer(1, False)

    row = lax.broadcasted_iota(jnp.int32, (ORB * ORB, ORB * ORB), 0)
    col = lax.broadcasted_iota(jnp.int32, (ORB * ORB, ORB * ORB), 1)
    coarse = jnp.floor((row.astype(F32) + 0.5) * (1.0 / ORB))
    source = (row.astype(F32) - coarse * ORB) * ORB + coarse
    keep = jnp.where(row == col, 1.0, 0.0).astype(BF)
    swap = jnp.where(source == col.astype(F32), 1.0, 0.0).astype(BF)
    block_map = jnp.concatenate(
        [dot_nt(keep, wb_ref[...]), dot_nt(swap, wb_ref[...])], axis=1
    ).astype(BF)

    wait_ghost(2)
    project(2)
    edge_layer(2, True)

    is_own = (lax.broadcasted_iota(jnp.int32, (NEIGH, 128), 0) & 2) == 0

    def widen(m, carry):
        halves = []
        for i in range(2):
            mine = last[pl.ds(2 * m + i, NEIGH, stride=ATOMS), :]
            halves.append(
                jnp.concatenate([jnp.where(is_own, mine, 0.0), jnp.where(is_own, 0.0, mine)], axis=1)
            )
        wide[pl.ds(pl.multiple_of(m * 144, 144), 144), :] = jnp.concatenate(halves, axis=0).astype(BF)
        return carry

    lax.fori_loop(0, ATOMS // 2, widen, 0)

    def block_step(c, carry):
        at = pl.multiple_of(c * 512, 512)
        blocks[:, pl.ds(at, 512)] = dot_nt(block_map, wide[pl.ds(at, 512), :]).astype(BF)
        return carry

    lax.fori_loop(0, SLOTS // 512, block_step, 0)

    def out_step(i, carry):
        start = pl.multiple_of(jnp.clip(i * 256 - 128, 0, SLOTS - 512), 128)
        at = pl.multiple_of(i * 256, 256)
        out_ref[:, pl.ds(at, 256)] = dot_nt(blocks[:, pl.ds(start, 512)], place[i]).astype(BF)
        return carry

    lax.fori_loop(0, SLOTS // 256, out_step, 0)

    for layer in range(LAYERS):
        for o in others:
            ghost_copy(layer, o).wait_send()
    for o in others:
        bond_copy(o).wait_send()


def shards(
    atom_feats,
    bond_embed,
    pair_dist,
    neighbours,
    slot_kind,
    own_rows,
    send_pos,
    recv_pos,
    w_left,
    w_right,
    w_edge_in,
    w_edge_out,
    w_msg,
    w_upd,
    node_gain,
    w_block,
):
    slots = neighbours | (slot_kind << 11) | ((recv_pos & 127) << 13)
    slots = jnp.tile(slots.reshape(ATOMS, NEIGH).T, (1, 2))
    dist = jnp.tile(pair_dist.reshape(ATOMS, NEIGH).T, (1, 2))
    owned = (own_rows // NEIGH) | ((own_rows % NEIGH) << 6) | (send_pos << 13)
    owned = owned.reshape(OFFSETS, 128)
    vmem = pl.BlockSpec(memory_space=pltpu.VMEM)
    return pl.pallas_call(
        kernel,
        out_shape=jax.ShapeDtypeStruct((ORB * ORB, SLOTS), BF),
        in_specs=[vmem] * 13,
        out_specs=vmem,
        scratch_shapes=[
            pltpu.VMEM((LAYERS, OFFSETS, ATOMS, 128), BF),
            pltpu.VMEM((LAYERS - 1, ATOMS, 128), BF),
            pltpu.VMEM((OFFSETS, CAP, 128), BF),
            pltpu.VMEM((OFFSETS, CAP, 128), BF),
            pltpu.VMEM((6, 24, 128), F32),
            pltpu.VMEM((OFFSETS, 128, 128), BF),
            pltpu.VMEM((128, OFFSETS * ATOMS), BF),
            pltpu.VMEM((OFFSETS, 128, 256), BF),
            pltpu.VMEM((OFFSETS * ATOMS, 128), BF),
            pltpu.VMEM((OFFSETS, 256, 128), BF),
            pltpu.VMEM((SLOTS, 128), F32),
            pltpu.VMEM((SLOTS, 256), BF),
            pltpu.VMEM((SLOTS // 256, 256, 512), BF),
            pltpu.VMEM((SLOTS, 128), F32),
            pltpu.VMEM((ORB * ORB, SLOTS), BF),
            pltpu.SemaphoreType.DMA((4, OFFSETS)),
            pltpu.SemaphoreType.DMA((4, OFFSETS)),
        ],
        compiler_params=pltpu.CompilerParams(
            collective_id=0, has_side_effects=True, vmem_limit_bytes=48 << 20
        ),
    )(
        atom_feats,
        bond_embed,
        slots,
        dist,
        owned,
        w_left,
        w_right,
        w_edge_in,
        w_edge_out,
        w_msg,
        w_upd,
        node_gain,
        w_block,
    )


def solution(mesh):
    spread = ("gx", "gy", "layer")
    placed = (P(spread, None), P(spread, None)) + (P(spread),) * 6 + (P(),) * 8
    return jax.shard_map(
        shards, mesh=mesh, in_specs=placed, out_specs=P(None, spread), check_vma=False
    )
```

```python
import jax
import jax.numpy as jnp
from jax import lax
from jax.experimental import pallas as pl
from jax.experimental.pallas import tpu as pltpu
from jax.sharding import PartitionSpec as P

ORB = 13
LAYERS = 3
OFFSETS = 18
SELF = 4
ATOMS = 64
NEIGH = 72
SLOTS = ATOMS * NEIGH
CAP = 128
LISTED = 2176
GROUP = 3
UNROLL = 1
MESH = pl.DeviceIdType.MESH
BF = jnp.bfloat16
F32 = jnp.float32
NT = (((1,), (1,)), ((), ()))


def dot(a, b):
    return jnp.dot(a, b, preferred_element_type=F32)


def dot_nt(a, b):
    return lax.dot_general(a, b, NT, preferred_element_type=F32)


def silu(v):
    half = 0.5 * v
    return half + half * jnp.tanh(half)


def reverse_of(offset):
    return offset // 9 * 9 + 8 - offset % 9


def kernel(
    *refs,
):
    sources, out_ref, held = refs[:16], refs[16], refs[17:33]
    (
        ghost,
        hidden,
        bond_send,
        bond_recv,
        line,
        rows,
        flat,
        pick_far,
        mix,
        tables,
        edge,
        last,
        wide,
        turned,
        place,
        blocks,
        in_sem,
        out_sem,
        send_sem,
        recv_sem,
    ) = refs[33:]
    (
        atom_ref,
        bond_ref,
        dist_ref,
        nbr_ref,
        kind_ref,
        own_ref,
        send_ref,
        recv_ref,
        wl_ref,
        wr_ref,
        wi_ref,
        wo_ref,
        wm_ref,
        wu_ref,
        gain_ref,
        wb_ref,
    ) = held
    gx, gy, sheet = lax.axis_index("gx"), lax.axis_index("gy"), lax.axis_index("layer")
    n_gx, n_gy = lax.axis_size("gx"), lax.axis_size("gy")

    def partner(offset):
        step_x = offset % 9 // 3 - 1
        step_y = offset % 3 - 1
        return (
            (gx + step_x + n_gx) % n_gx,
            (gy + step_y + n_gy) % n_gy,
            (sheet + offset // 9) % 2,
        )

    others = [0, 2, 6, 8, 9, 11, 15, 17, 3, 5, 12, 14, 1, 7, 10, 16, 13]

    barrier = pltpu.get_barrier_semaphore()
    for o in others:
        pl.semaphore_signal(barrier, inc=1, device_id=partner(o), device_id_type=MESH)
    fetches = [
        pltpu.make_async_copy(source, target, in_sem.at[i])
        for i, (source, target) in enumerate(zip(sources, held))
    ]
    for i in (5, 6, 3, 4, 7, 2, 0, 1, 12, 13, 14, 8, 9, 10, 11, 15):
        fetches[i].start()
    def ghost_copy(layer, o):
        source = atom_ref if layer == 0 else hidden.at[layer - 1]
        return pltpu.make_async_remote_copy(
            src_ref=source,
            dst_ref=ghost.at[layer, reverse_of(o)],
            send_sem=send_sem.at[layer, o],
            recv_sem=recv_sem.at[layer, reverse_of(o)],
            device_id=partner(o),
            device_id_type=MESH,
        )

    def bond_copy(o):
        return pltpu.make_async_remote_copy(
            src_ref=bond_send.at[o],
            dst_ref=bond_recv.at[reverse_of(o)],
            send_sem=send_sem.at[3, o],
            recv_sem=recv_sem.at[3, reverse_of(o)],
            device_id=partner(o),
            device_id_type=MESH,
        )

    for i in (5, 6, 3, 4, 7, 2):
        fetches[i].wait()

    sub = lax.broadcasted_iota(jnp.int32, (128, 128), 0)
    lane1 = lax.broadcasted_iota(jnp.int32, (1, 128), 1)
    packed = (nbr_ref[...] | (kind_ref[...] << 11) | ((recv_ref[...] & 127) << 13)).astype(F32)
    flat[0 : SLOTS // 128, :] = packed

    def by_slot(source, k):
        for n in range(ATOMS):
            at, first = n * NEIGH // 128, n * NEIGH % 128
            mine = source[at : at + 1, :]
            if first + NEIGH > 128:
                mine = jnp.where(lane1 >= first, mine, source[at + 1 : at + 2, :])
            line[k, n : n + 1, :] = mine
        moved = jnp.concatenate([line[k], line[k]], axis=0)
        for bit in (1, 2, 4, 8):
            moved = jnp.where((sub * 7 & bit) != 0, pltpu.roll(moved, 8 * bit, 1), moved)
        return moved.T[:NEIGH, :]

    slot = by_slot(flat, 0).astype(jnp.int32)
    nbr, kind, place_in = slot & 2047, (slot >> 11) & 3, slot >> 13
    offset_of = nbr >> 6
    atom_of = ((nbr & 63) + 1).astype(F32)
    scaled = by_slot(dist_ref, 1) / 7.0
    falloff = 1.0 - scaled * scaled
    env = jnp.where(kind > 0, falloff * falloff, 0.0)
    own_key = jnp.where(kind == 1, offset_of, -1)
    far_key = jnp.where(kind == 2, offset_of, -1)
    recv_place = (place_in + 1).astype(F32)

    sub72 = lax.broadcasted_iota(jnp.int32, (NEIGH, 128), 0)
    send_place = jnp.zeros((NEIGH, 128), F32)
    own_rows = own_ref[...].astype(F32)
    own_atom = jnp.floor((own_rows + 0.5) * (1.0 / NEIGH))
    own_slot = own_rows - own_atom * NEIGH
    own_place = ((send_ref[...] & 127) + 1).astype(F32)
    sub_slot, sub_atom = sub72.astype(F32), (sub & 63).astype(F32)
    for k in range(OFFSETS):
        at_slot = jnp.where(own_slot[k : k + 1, :] == sub_slot, 1.0, 0.0).astype(BF)
        at_atom = jnp.where(own_atom[k : k + 1, :] == sub_atom, own_place[k : k + 1, :], 0.0)
        send_place = send_place + dot_nt(at_slot, at_atom.astype(BF))

    before = jnp.where(
        lax.broadcasted_iota(jnp.int32, (NEIGH, NEIGH), 0)
        > lax.broadcasted_iota(jnp.int32, (NEIGH, NEIGH), 1),
        1.0,
        0.0,
    ).astype(BF)
    rank_lane = (lax.broadcasted_iota(jnp.int32, (NEIGH, 128), 1) >> 6).astype(F32)

    def total(v):
        return jnp.sum(v, axis=0, keepdims=True)

    def tables_step(o, where_to):
        own = jnp.where(own_key == o, 1.0, 0.0)
        far = jnp.where(far_key == o, 1.0, 0.0)
        count = dot(before, jnp.concatenate([own, far], axis=1).astype(BF))
        own_rank, far_rank = count[:, :128], count[:, 128:]
        own_hit = jnp.where(own_rank == rank_lane, own, 0.0)
        far_hit = jnp.where(far_rank == rank_lane, far, 0.0)
        rows[0, pl.ds(o, 1), :] = total(own_hit * atom_of) - 1.0
        rows[1, pl.ds(o, 1), :] = total(far_hit * atom_of) - 1.0
        rows[2, pl.ds(o, 1), :] = total(own_hit * send_place) - 1.0
        rows[3, pl.ds(o, 1), :] = total(far_hit * recv_place) - 1.0
        rows[4, pl.ds(o, 1), :] = total(own_hit * env)
        rows[5, pl.ds(o, 1), :] = total(far_hit * env)
        base = (4 * o + 1).astype(F32)
        return where_to + own * (own_rank + base) + far * (far_rank + (base + 2.0))

    where_to = lax.fori_loop(0, OFFSETS, tables_step, jnp.zeros((NEIGH, 128), F32), unroll=6)

    subf = (sub & 63).astype(F32)
    for g in range(OFFSETS // 2):
        low = sub < 64

        def pair(kind_of_row):
            first = rows[kind_of_row, 2 * g : 2 * g + 1, :]
            second = rows[kind_of_row, 2 * g + 1 : 2 * g + 2, :]
            return jnp.where(low, first, second)

        weights = jnp.where(pair(0) == subf, pair(4), 0.0) + jnp.where(
            pair(1) == subf, pair(5), 0.0
        )
        mix[:, g * 128 : (g + 1) * 128] = weights.T.astype(BF)

    def far_step(o, carry):
        own_atom, far_atom = rows[0, pl.ds(o, 1), :], rows[1, pl.ds(o, 1), :]
        wanted = jnp.where(sub < 64, own_atom, far_atom)
        pick_far[o] = jnp.where(wanted == subf, 1.0, 0.0).astype(BF).T
        return carry

    lax.fori_loop(0, OFFSETS, far_step, 0, unroll=6)
    fetches[0].wait()

    pl.semaphore_wait(barrier, len(others))
    for o in others:
        ghost_copy(0, o).start()
    ghost[0, SELF] = atom_ref[...]

    sub384 = lax.broadcasted_iota(jnp.int32, (384, 128), 0)

    def bond_step(step, carry):
        first = step * 384
        picked = [
            jnp.where(send_ref[k : k + 1, :] - first == sub384, 1.0, 0.0).astype(BF)
            for k in range(LISTED // 128)
        ]
        got = dot(jnp.concatenate(picked, axis=1), bond_ref[:LISTED, :]).astype(BF)
        for i in range(3):
            o = step * 3 + i
            bond_send[o] = got[i * 128 : (i + 1) * 128, :]

            @pl.when(o != SELF)
            def _():
                bond_copy(o).start()

        return carry

    fetches[1].wait()
    lax.fori_loop(0, OFFSETS // 3, bond_step, 0)

    def wait_ghost(layer):
        for o in others:
            pltpu.make_async_remote_copy(
                src_ref=ghost.at[layer, o],
                dst_ref=ghost.at[layer, o],
                send_sem=send_sem.at[layer, o],
                recv_sem=recv_sem.at[layer, o],
                device_id=partner(o),
                device_id_type=MESH,
            ).wait_recv()

    def update_hidden(layer):
        two = dot(mix[...], ghost[layer].reshape(OFFSETS * ATOMS, 128))
        reached = (two[:ATOMS] + two[ATOMS:]).astype(BF)
        summed = (dot(reached, wm_ref[layer]) * 0.125).astype(BF)
        updated = ghost[layer, SELF].astype(F32) + silu(dot(summed, wu_ref[layer]))
        mean = jnp.mean(updated * updated, axis=-1, keepdims=True)
        fresh = updated * lax.rsqrt(mean + 1e-06) * gain_ref[layer : layer + 1, :]
        hidden[layer] = fresh.astype(BF)
        for o in others:
            ghost_copy(layer + 1, o).start()
        ghost[layer + 1, SELF] = fresh.astype(BF)

    def project(layer):
        both = jnp.concatenate([wr_ref[layer], wl_ref[layer]], axis=1)

        got = dot(ghost[layer].reshape(OFFSETS * ATOMS, 128), both).astype(BF)
        for o in range(OFFSETS):
            tables[o, 0:64, 0:128] = got[o * 64 : (o + 1) * 64, :128]
            tables[o, 64:128, 128:256] = got[o * 64 : (o + 1) * 64, 128:]

    def twice(w):
        none = jnp.zeros_like(w)
        return jnp.concatenate(
            [jnp.concatenate([w, none], axis=1), jnp.concatenate([none, w], axis=1)], axis=0
        )

    averages = twice(jnp.full((128, 128), 1.0 / 128.0, BF))

    def edge_layer(layer, final):
        right = tables[SELF, 0:64, 0:128].astype(F32)
        left = tables[SELF, 64:128, 128:256].astype(F32)
        near = jnp.concatenate([left, right], axis=1)
        near = jnp.concatenate([near, near] * GROUP, axis=0)
        edge_in, edge_out = twice(wi_ref[layer]), twice(wo_ref[layer])

        def one(step, carry):
            state = edge[pl.ds(step * GROUP, GROUP)].reshape(GROUP * 128, 256)
            inner = dot(state, edge_in)
            reached = [
                dot(pick_far[step * GROUP + i], tables[step * GROUP + i]) for i in range(GROUP)
            ]
            product = jnp.concatenate(reached, axis=0) * near
            gate = silu(inner * product).astype(BF)
            renewed = state.astype(F32) + dot(gate, edge_out)
            mean = dot((renewed * renewed).astype(BF), averages)
            fresh = renewed * lax.rsqrt(mean + 1e-06)
            if final:
                for i in range(GROUP):
                    at = (step * GROUP + i) * 256
                    last[pl.ds(at, 128), :] = fresh[i * 128 : (i + 1) * 128, :128]
                    last[pl.ds(at + 128, 128), :] = fresh[i * 128 : (i + 1) * 128, 128:]
            else:
                edge[pl.ds(step * GROUP, GROUP)] = fresh.astype(BF).reshape(GROUP, 128, 256)
            return carry

        lax.fori_loop(0, OFFSETS // GROUP, one, 0, unroll=UNROLL)

    subq = sub.astype(F32)

    def own_step(o, carry):
        picker = jnp.where(rows[2, pl.ds(o, 1), :] == subq, 1.0, 0.0).astype(BF).T
        edge[o, :, 0:128] = dot(picker, bond_send[o]).astype(BF)
        return carry

    lax.fori_loop(0, OFFSETS, own_step, 0, unroll=6)

    atom_lane = ((lax.broadcasted_iota(jnp.int32, (NEIGH, 128), 1) & 63) * NEIGH - 1).astype(F32)
    column = jnp.where(where_to > 0.0, where_to + atom_lane, -1.0)
    column = jnp.concatenate([column, jnp.full((128 - NEIGH, 128), -1.0, F32)], axis=0).T
    column = pltpu.roll(column, 0, 1, stride=NEIGH - 64, stride_axis=0)
    column = jnp.where((sub & 1) == 1, pltpu.roll(column, 64, 1), column)
    for c in range(SLOTS // 128):
        first, final = c * 128 // NEIGH, (c * 128 + 127) // NEIGH
        found = column[first : first + 1, :]
        for n in range(first + 1, final + 1):
            found = jnp.where(lane1 >= n * NEIGH - c * 128, column[n : n + 1, :], found)
        flat[c : c + 1, :] = found

    def place_step(i, carry):
        base = i // 9 * (SLOTS // 2)
        start = base + jnp.clip(i % 9 * 256 - 128, 0, SLOTS // 2 - 512)
        here = (lax.broadcasted_iota(jnp.int32, (512, 128), 0) + start).astype(F32)
        for k in range(2):
            wanted = flat[pl.ds(2 * i + k, 1), :]
            place[i, :, k * 128 : (k + 1) * 128] = jnp.where(here == wanted, 1.0, 0.0).astype(BF)
        return carry

    lax.fori_loop(0, SLOTS // 256, place_step, 0)

    tables[...] = jnp.zeros_like(tables)
    for i in (12, 13, 14):
        fetches[i].wait()
    wait_ghost(0)
    update_hidden(0)

    for i in (8, 9, 10, 11, 15):
        fetches[i].wait()
    project(0)
    for o in others:
        pltpu.make_async_remote_copy(
            src_ref=bond_recv.at[o],
            dst_ref=bond_recv.at[o],
            send_sem=send_sem.at[3, o],
            recv_sem=recv_sem.at[3, o],
            device_id=partner(o),
            device_id_type=MESH,
        ).wait_recv()
    bond_recv[SELF] = bond_send[SELF]

    def recv_step(o, carry):
        picker = jnp.where(rows[3, pl.ds(o, 1), :] == subq, 1.0, 0.0).astype(BF).T
        edge[o, :, 128:256] = dot(picker, bond_recv[o]).astype(BF)
        return carry

    lax.fori_loop(0, OFFSETS, recv_step, 0, unroll=6)
    edge_layer(0, False)

    wait_ghost(1)
    update_hidden(1)
    project(1)
    edge_layer(1, False)

    row = lax.broadcasted_iota(jnp.int32, (ORB * ORB, ORB * ORB), 0)
    col = lax.broadcasted_iota(jnp.int32, (ORB * ORB, ORB * ORB), 1)
    coarse = jnp.floor((row.astype(F32) + 0.5) * (1.0 / ORB))
    source = (row.astype(F32) - coarse * ORB) * ORB + coarse
    swap = jnp.where(source == col.astype(F32), 1.0, 0.0).astype(BF)
    block_map = jnp.concatenate([wb_ref[...], dot(swap, wb_ref[...]).astype(BF)], axis=1)

    wait_ghost(2)
    project(2)
    edge_layer(2, True)

    is_own = (lax.broadcasted_iota(jnp.int32, (128, 128), 1) & 2) == 0
    half = SLOTS // 2

    def gather_half(h):
        for m in range(h * 16, h * 16 + 16):
            mine = [last[pl.ds(2 * m + i, NEIGH, stride=ATOMS), :] for i in range(2)]
            wide[m * 144 : m * 144 + 144, :] = jnp.concatenate(mine, axis=0).astype(BF)
        for c in range(h * 18, h * 18 + 18):
            at = c * 128
            mine = wide[at : at + 128, :].T.astype(F32)
            turned[0:128, at : at + 128] = jnp.where(is_own, mine, 0.0).astype(BF)
            turned[128:256, at : at + 128] = jnp.where(is_own, 0.0, mine).astype(BF)

    def block_half(h):
        for c in range(3):
            at = h * half + c * 768
            blocks[:, at : at + 768] = dot(block_map, turned[:, at : at + 768]).astype(BF)

    def out_half(h):
        for i in range(9):
            start = h * half + min(max(i * 256 - 128, 0), half - 512)
            at = h * half + i * 256
            out_ref[:, at : at + 256] = dot(
                blocks[:, start : start + 512], place[h * 9 + i]
            ).astype(BF)

    gather_half(0)
    block_half(0)
    gather_half(1)
    out_half(0)
    block_half(1)
    out_half(1)

    for layer in range(LAYERS):
        for o in others:
            ghost_copy(layer, o).wait_send()
    for o in others:
        bond_copy(o).wait_send()


def shards(
    atom_feats,
    bond_embed,
    pair_dist,
    neighbours,
    slot_kind,
    own_rows,
    send_pos,
    recv_pos,
    w_left,
    w_right,
    w_edge_in,
    w_edge_out,
    w_msg,
    w_upd,
    node_gain,
    w_block,
):
    hbm, vmem = pl.BlockSpec(memory_space=pltpu.HBM), pl.BlockSpec(memory_space=pltpu.VMEM)
    operands = (
        atom_feats,
        bond_embed,
        pair_dist.reshape(SLOTS // 128, 128),
        neighbours.reshape(SLOTS // 128, 128),
        slot_kind.reshape(SLOTS // 128, 128),
        own_rows.reshape(OFFSETS, 128),
        send_pos.reshape(OFFSETS, 128),
        recv_pos.reshape(SLOTS // 128, 128),
        w_left,
        w_right,
        w_edge_in,
        w_edge_out,
        w_msg,
        w_upd,
        node_gain,
        w_block.T,
    )
    return pl.pallas_call(
        kernel,
        out_shape=jax.ShapeDtypeStruct((ORB * ORB, SLOTS), BF),
        in_specs=[hbm] * len(operands),
        out_specs=vmem,
        scratch_shapes=[pltpu.VMEM(v.shape, v.dtype) for v in operands]
        + [
            pltpu.VMEM((LAYERS, OFFSETS, ATOMS, 128), BF),
            pltpu.VMEM((LAYERS - 1, ATOMS, 128), BF),
            pltpu.VMEM((OFFSETS, CAP, 128), BF),
            pltpu.VMEM((OFFSETS, CAP, 128), BF),
            pltpu.VMEM((2, ATOMS, 128), F32),
            pltpu.VMEM((6, 24, 128), F32),
            pltpu.VMEM((40, 128), F32),
            pltpu.VMEM((OFFSETS, 128, 128), BF),
            pltpu.VMEM((128, OFFSETS * ATOMS), BF),
            pltpu.VMEM((OFFSETS, 128, 256), BF),
            pltpu.VMEM((OFFSETS, 128, 256), BF),
            pltpu.VMEM((SLOTS, 128), F32),
            pltpu.VMEM((SLOTS, 128), BF),
            pltpu.VMEM((256, SLOTS), BF),
            pltpu.VMEM((SLOTS // 256, 512, 256), BF),
            pltpu.VMEM((ORB * ORB, SLOTS), BF),
            pltpu.SemaphoreType.DMA((len(operands),)),
            pltpu.SemaphoreType.DMA((1,)),
            pltpu.SemaphoreType.DMA((4, OFFSETS)),
            pltpu.SemaphoreType.DMA((4, OFFSETS)),
        ],
        compiler_params=pltpu.CompilerParams(
            collective_id=0, has_side_effects=True, vmem_limit_bytes=60 << 20
        ),
    )(*operands)


def solution(mesh):
    spread = ("gx", "gy", "layer")
    placed = (P(spread, None), P(spread, None)) + (P(spread),) * 6 + (P(),) * 8
    return jax.shard_map(
        shards, mesh=mesh, in_specs=placed, out_specs=P(None, spread), check_vma=False
    )
```

```python
import jax
import jax.numpy as jnp
from jax import lax
from jax.experimental import pallas as pl
from jax.experimental.pallas import tpu as pltpu
from jax.sharding import PartitionSpec as P

ORB = 13
LAYERS = 3
OFFSETS = 18
SELF = 4
ATOMS = 64
NEIGH = 72
SLOTS = ATOMS * NEIGH
CAP = 128
LISTED = 2176
MESH = pl.DeviceIdType.MESH
BF = jnp.bfloat16
F32 = jnp.float32
NT = (((1,), (1,)), ((), ()))


def dot(a, b):
    return jnp.dot(a, b, preferred_element_type=F32)


def dot_nt(a, b):
    return lax.dot_general(a, b, NT, preferred_element_type=F32)


def silu(v):
    half = 0.5 * v
    return half + half * jnp.tanh(half)


def reverse_of(offset):
    return offset // 9 * 9 + 8 - offset % 9


def kernel(
    *refs,
):
    sources, out_ref, held = refs[:16], refs[16], refs[17:33]
    (
        ghost,
        hidden,
        bond_send,
        bond_recv,
        line,
        rows,
        flat,
        pick_far,
        mix,
        tables,
        edge,
        last,
        wide,
        spread,
        place,
        result,
        in_sem,
        out_sem,
        send_sem,
        recv_sem,
    ) = refs[33:]
    (
        atom_ref,
        bond_ref,
        dist_ref,
        nbr_ref,
        kind_ref,
        own_ref,
        send_ref,
        recv_ref,
        wl_ref,
        wr_ref,
        wi_ref,
        wo_ref,
        wm_ref,
        wu_ref,
        gain_ref,
        wb_ref,
    ) = held
    gx, gy, sheet = lax.axis_index("gx"), lax.axis_index("gy"), lax.axis_index("layer")
    n_gx, n_gy = lax.axis_size("gx"), lax.axis_size("gy")

    def partner(offset):
        step_x = offset % 9 // 3 - 1
        step_y = offset % 3 - 1
        return (
            (gx + step_x + n_gx) % n_gx,
            (gy + step_y + n_gy) % n_gy,
            (sheet + offset // 9) % 2,
        )

    others = [0, 2, 6, 8, 9, 11, 15, 17, 3, 5, 12, 14, 1, 7, 10, 16, 13]

    barrier = pltpu.get_barrier_semaphore()
    for o in others:
        pl.semaphore_signal(barrier, inc=1, device_id=partner(o), device_id_type=MESH)
    fetches = [
        pltpu.make_async_copy(source, target, in_sem.at[i])
        for i, (source, target) in enumerate(zip(sources, held))
    ]
    for i in (5, 6, 3, 4, 7, 2, 0, 1, 12, 13, 14, 8, 9, 10, 11, 15):
        fetches[i].start()
    def ghost_copy(layer, o):
        source = atom_ref if layer == 0 else hidden.at[layer - 1]
        return pltpu.make_async_remote_copy(
            src_ref=source,
            dst_ref=ghost.at[layer, reverse_of(o)],
            send_sem=send_sem.at[layer],
            recv_sem=recv_sem.at[layer],
            device_id=partner(o),
            device_id_type=MESH,
        )

    def bond_copy(o):
        return pltpu.make_async_remote_copy(
            src_ref=bond_send.at[o],
            dst_ref=bond_recv.at[reverse_of(o)],
            send_sem=send_sem.at[3],
            recv_sem=recv_sem.at[3],
            device_id=partner(o),
            device_id_type=MESH,
        )

    for i in (5, 6, 3, 4, 7, 2):
        fetches[i].wait()

    sub = lax.broadcasted_iota(jnp.int32, (128, 128), 0)
    lane1 = lax.broadcasted_iota(jnp.int32, (1, 128), 1)
    packed = (nbr_ref[...] | (kind_ref[...] << 11) | ((recv_ref[...] & 127) << 13)).astype(F32)
    flat[0 : SLOTS // 128, :] = packed

    def by_slot(source, k):
        for n in range(ATOMS):
            at, first = n * NEIGH // 128, n * NEIGH % 128
            mine = source[at : at + 1, :]
            if first + NEIGH > 128:
                mine = jnp.where(lane1 >= first, mine, source[at + 1 : at + 2, :])
            line[k, n : n + 1, :] = mine
        moved = jnp.concatenate([line[k], line[k]], axis=0)
        for bit in (1, 2, 4, 8):
            moved = jnp.where((sub * 7 & bit) != 0, pltpu.roll(moved, 8 * bit, 1), moved)
        return moved.T[:NEIGH, :]

    slot = by_slot(flat, 0).astype(jnp.int32)
    nbr, kind, place_in = slot & 2047, (slot >> 11) & 3, slot >> 13
    offset_of = nbr >> 6
    atom_of = ((nbr & 63) + 1).astype(F32)
    scaled = by_slot(dist_ref, 1) / 7.0
    falloff = 1.0 - scaled * scaled
    env = jnp.where(kind > 0, falloff * falloff, 0.0)
    own_key = jnp.where(kind == 1, offset_of, -1)
    far_key = jnp.where(kind == 2, offset_of, -1)
    recv_place = (place_in + 1).astype(F32)

    sub72 = lax.broadcasted_iota(jnp.int32, (NEIGH, 128), 0)
    send_place = jnp.zeros((NEIGH, 128), F32)
    own_rows = own_ref[...].astype(F32)
    own_atom = jnp.floor((own_rows + 0.5) * (1.0 / NEIGH))
    own_slot = own_rows - own_atom * NEIGH
    own_place = ((send_ref[...] & 127) + 1).astype(F32)
    sub_slot, sub_atom = sub72.astype(F32), (sub & 63).astype(F32)
    for k in range(OFFSETS):
        at_slot = jnp.where(own_slot[k : k + 1, :] == sub_slot, 1.0, 0.0).astype(BF)
        at_atom = jnp.where(own_atom[k : k + 1, :] == sub_atom, own_place[k : k + 1, :], 0.0)
        send_place = send_place + dot_nt(at_slot, at_atom.astype(BF))

    before = jnp.where(
        lax.broadcasted_iota(jnp.int32, (NEIGH, NEIGH), 0)
        > lax.broadcasted_iota(jnp.int32, (NEIGH, NEIGH), 1),
        1.0,
        0.0,
    ).astype(BF)
    rank_lane = (lax.broadcasted_iota(jnp.int32, (NEIGH, 128), 1) >> 6).astype(F32)

    def total(v):
        return jnp.sum(v, axis=0, keepdims=True)

    def tables_step(o, where_to):
        own = jnp.where(own_key == o, 1.0, 0.0)
        far = jnp.where(far_key == o, 1.0, 0.0)
        count = dot(before, jnp.concatenate([own, far], axis=1).astype(BF))
        own_rank, far_rank = count[:, :128], count[:, 128:]
        own_hit = jnp.where(own_rank == rank_lane, own, 0.0)
        far_hit = jnp.where(far_rank == rank_lane, far, 0.0)
        rows[0, pl.ds(o, 1), :] = total(own_hit * atom_of) - 1.0
        rows[1, pl.ds(o, 1), :] = total(far_hit * atom_of) - 1.0
        rows[2, pl.ds(o, 1), :] = total(own_hit * send_place) - 1.0
        rows[3, pl.ds(o, 1), :] = total(far_hit * recv_place) - 1.0
        rows[4, pl.ds(o, 1), :] = total(own_hit * env)
        rows[5, pl.ds(o, 1), :] = total(far_hit * env)
        base = (4 * o + 1).astype(F32)
        return where_to + own * (own_rank + base) + far * (far_rank + (base + 2.0))

    where_to = lax.fori_loop(0, OFFSETS, tables_step, jnp.zeros((NEIGH, 128), F32), unroll=6)

    subf = (sub & 63).astype(F32)
    for g in range(OFFSETS // 2):
        low = sub < 64

        def pair(kind_of_row):
            first = rows[kind_of_row, 2 * g : 2 * g + 1, :]
            second = rows[kind_of_row, 2 * g + 1 : 2 * g + 2, :]
            return jnp.where(low, first, second)

        weights = jnp.where(pair(0) == subf, pair(4), 0.0) + jnp.where(
            pair(1) == subf, pair(5), 0.0
        )
        mix[:, g * 128 : (g + 1) * 128] = weights.T.astype(BF)

    def far_step(o, carry):
        own_atom, far_atom = rows[0, pl.ds(o, 1), :], rows[1, pl.ds(o, 1), :]
        wanted = jnp.where(sub < 64, own_atom, far_atom)
        pick_far[o] = jnp.where(wanted == subf, 1.0, 0.0).astype(BF).T
        return carry

    lax.fori_loop(0, OFFSETS, far_step, 0, unroll=6)
    fetches[0].wait()

    pl.semaphore_wait(barrier, len(others))
    for o in others:
        ghost_copy(0, o).start()
    ghost[0, SELF] = atom_ref[...]

    sub384 = lax.broadcasted_iota(jnp.int32, (384, 128), 0)

    def bond_step(step, carry):
        first = step * 384
        picked = [
            jnp.where(send_ref[k : k + 1, :] - first == sub384, 1.0, 0.0).astype(BF)
            for k in range(LISTED // 128)
        ]
        got = dot(jnp.concatenate(picked, axis=1), bond_ref[:LISTED, :]).astype(BF)
        for i in range(3):
            o = step * 3 + i
            bond_send[o] = got[i * 128 : (i + 1) * 128, :]

            @pl.when(o != SELF)
            def _():
                bond_copy(o).start()

        return carry

    fetches[1].wait()
    lax.fori_loop(0, OFFSETS // 3, bond_step, 0)

    def exchange(k):
        mine = bond_recv if k == 3 else ghost.at[k]
        whole = mine.at[pl.ds(0, len(others))]
        return pltpu.make_async_remote_copy(
            src_ref=whole,
            dst_ref=whole,
            send_sem=send_sem.at[k],
            recv_sem=recv_sem.at[k],
            device_id=partner(0),
            device_id_type=MESH,
        )

    def wait_ghost(layer):
        exchange(layer).wait_recv()

    def update_hidden(layer):
        two = dot(mix[...], ghost[layer].reshape(OFFSETS * ATOMS, 128))
        reached = (two[:ATOMS] + two[ATOMS:]).astype(BF)
        summed = (dot(reached, wm_ref[layer]) * 0.125).astype(BF)
        updated = ghost[layer, SELF].astype(F32) + silu(dot(summed, wu_ref[layer]))
        mean = jnp.mean(updated * updated, axis=-1, keepdims=True)
        fresh = updated * lax.rsqrt(mean + 1e-06) * gain_ref[layer : layer + 1, :]
        hidden[layer] = fresh.astype(BF)
        for o in others:
            ghost_copy(layer + 1, o).start()
        ghost[layer + 1, SELF] = fresh.astype(BF)

    def project(layer):
        both = jnp.concatenate([wr_ref[layer], wl_ref[layer]], axis=1)

        got = dot(ghost[layer].reshape(OFFSETS * ATOMS, 128), both).astype(BF)
        for o in range(OFFSETS):
            tables[o, 0:64, 0:128] = got[o * 64 : (o + 1) * 64, :128]
            tables[o, 64:128, 128:256] = got[o * 64 : (o + 1) * 64, 128:]

    def twice(w):
        none = jnp.zeros_like(w)
        return jnp.concatenate(
            [jnp.concatenate([w, none], axis=1), jnp.concatenate([none, w], axis=1)], axis=0
        )

    averages = twice(jnp.full((128, 128), 1.0 / 128.0, BF))

    def edge_inner(layer):
        return dot(edge[...].reshape(OFFSETS * 128, 256), twice(wi_ref[layer]))

    def edge_layer(layer, final, inner):
        right = tables[SELF, 0:64, 0:128].astype(F32)
        left = tables[SELF, 64:128, 128:256].astype(F32)
        near = jnp.concatenate([left, right], axis=1)
        near = jnp.concatenate([near, near] * OFFSETS, axis=0)
        state = edge[...].reshape(OFFSETS * 128, 256)
        reached = [dot(pick_far[o], tables[o]) for o in range(OFFSETS)]
        gate = silu(inner * (jnp.concatenate(reached, axis=0) * near)).astype(BF)
        renewed = state.astype(F32) + dot(gate, twice(wo_ref[layer]))
        mean = dot((renewed * renewed).astype(BF), averages)
        fresh = renewed * lax.rsqrt(mean + 1e-06)
        if final:
            for o in range(OFFSETS):
                mine = fresh[o * 128 : (o + 1) * 128, :]
                last[o * 256 : o * 256 + 128, :] = mine[:, :128]
                last[o * 256 + 128 : o * 256 + 256, :] = mine[:, 128:]
        else:
            edge[...] = fresh.astype(BF).reshape(OFFSETS, 128, 256)

    subq = sub.astype(F32)

    def own_step(o, carry):
        picker = jnp.where(rows[2, pl.ds(o, 1), :] == subq, 1.0, 0.0).astype(BF).T
        edge[o, :, 0:128] = dot(picker, bond_send[o]).astype(BF)
        return carry

    lax.fori_loop(0, OFFSETS, own_step, 0, unroll=6)

    for n in range(ATOMS):
        place_of = jnp.broadcast_to(where_to[:, n : n + 1], (NEIGH, 128))
        spread[n * NEIGH : (n + 1) * NEIGH, :] = jnp.where(
            place_of > 0.0, place_of + (n % 32 * NEIGH - 1.0), -1.0
        )

    def place_step(i, carry):
        start = jnp.clip(i % 9 * 256 - 128, 0, SLOTS // 2 - 512)
        wanted = spread[pl.ds(pl.multiple_of(i * 256, 256), 256), :]
        for k in range(4):
            here = lax.broadcasted_iota(jnp.int32, (256, 128), 1) + (start + k * 128)
            place[i, :, k * 128 : (k + 1) * 128] = jnp.where(
                wanted == here.astype(F32), 1.0, 0.0
            ).astype(BF)
        return carry

    lax.fori_loop(0, SLOTS // 256, place_step, 0, unroll=2)

    tables[...] = jnp.zeros_like(tables)
    for i in (12, 13, 14):
        fetches[i].wait()
    wait_ghost(0)
    update_hidden(0)

    for i in (8, 9, 10, 11, 15):
        fetches[i].wait()
    project(0)
    wait_ghost(1)
    update_hidden(1)

    exchange(3).wait_recv()
    bond_recv[SELF] = bond_send[SELF]

    def recv_step(o, carry):
        picker = jnp.where(rows[3, pl.ds(o, 1), :] == subq, 1.0, 0.0).astype(BF).T
        edge[o, :, 128:256] = dot(picker, bond_recv[o]).astype(BF)
        return carry

    lax.fori_loop(0, OFFSETS, recv_step, 0, unroll=6)
    edge_layer(0, False, edge_inner(0))

    project(1)
    edge_layer(1, False, edge_inner(1))
    inner = edge_inner(2)

    row = lax.broadcasted_iota(jnp.int32, (ORB * ORB, ORB * ORB), 0)
    col = lax.broadcasted_iota(jnp.int32, (ORB * ORB, ORB * ORB), 1)
    coarse = jnp.floor((row.astype(F32) + 0.5) * (1.0 / ORB))
    source = (row.astype(F32) - coarse * ORB) * ORB + coarse
    swap = jnp.where(source == col.astype(F32), 1.0, 0.0).astype(BF)
    block_map = jnp.concatenate([wb_ref[...], dot(swap, wb_ref[...]).astype(BF)], axis=1)

    wait_ghost(2)
    project(2)
    edge_layer(2, True, inner)

    half = SLOTS // 2

    def write(c):
        columns = pl.ds(c * 768, 768)
        return pltpu.make_async_copy(
            result.at[:, columns], out_ref.at[:, columns], out_sem.at[c]
        )

    for h in range(2):
        for m in range(h * 16, h * 16 + 16):
            mine = [last[pl.ds(2 * m + i, NEIGH, stride=ATOMS), :] for i in range(2)]
            wide[m * 144 : m * 144 + 144, :] = jnp.concatenate(mine, axis=0).astype(BF)
    for h in range(2):
        states = []
        for i in range(9):
            start = h * half + min(max(i * 256 - 128, 0), half - 512)
            states.append(dot(place[h * 9 + i], wide[start : start + 512, :]).astype(BF).T)
        for i in range(9):
            at = h * half + i * 256
            kinds = [kind_ref[at // 128 + k : at // 128 + k + 1, :] for k in range(2)]
            kinds = jnp.concatenate(kinds, axis=1)
            state = states[i].astype(F32)
            stacked = [jnp.where(kinds == k, state, 0.0).astype(BF) for k in (1, 2)]
            result[:, at : at + 256] = dot(block_map, jnp.concatenate(stacked, axis=0)).astype(BF)
            if i % 3 == 2:
                write(h * 3 + i // 3).start()

    for c in range(6):
        write(c).wait()
    for k in range(4):
        exchange(k).wait_send()


def shards(
    atom_feats,
    bond_embed,
    pair_dist,
    neighbours,
    slot_kind,
    own_rows,
    send_pos,
    recv_pos,
    w_left,
    w_right,
    w_edge_in,
    w_edge_out,
    w_msg,
    w_upd,
    node_gain,
    w_block,
):
    hbm = pl.BlockSpec(memory_space=pltpu.HBM)
    operands = (
        atom_feats,
        bond_embed,
        pair_dist.reshape(SLOTS // 128, 128),
        neighbours.reshape(SLOTS // 128, 128),
        slot_kind.reshape(SLOTS // 128, 128),
        own_rows.reshape(OFFSETS, 128),
        send_pos.reshape(OFFSETS, 128),
        recv_pos.reshape(SLOTS // 128, 128),
        w_left,
        w_right,
        w_edge_in,
        w_edge_out,
        w_msg,
        w_upd,
        node_gain,
        w_block.T,
    )
    return pl.pallas_call(
        kernel,
        out_shape=jax.ShapeDtypeStruct((ORB * ORB, SLOTS), BF),
        in_specs=[hbm] * len(operands),
        out_specs=hbm,
        scratch_shapes=[pltpu.VMEM(v.shape, v.dtype) for v in operands]
        + [
            pltpu.VMEM((LAYERS, OFFSETS, ATOMS, 128), BF),
            pltpu.VMEM((LAYERS - 1, ATOMS, 128), BF),
            pltpu.VMEM((OFFSETS, CAP, 128), BF),
            pltpu.VMEM((OFFSETS, CAP, 128), BF),
            pltpu.VMEM((2, ATOMS, 128), F32),
            pltpu.VMEM((6, 24, 128), F32),
            pltpu.VMEM((40, 128), F32),
            pltpu.VMEM((OFFSETS, 128, 128), BF),
            pltpu.VMEM((128, OFFSETS * ATOMS), BF),
            pltpu.VMEM((OFFSETS, 128, 256), BF),
            pltpu.VMEM((OFFSETS, 128, 256), BF),
            pltpu.VMEM((SLOTS, 128), F32),
            pltpu.VMEM((SLOTS, 128), BF),
            pltpu.VMEM((SLOTS, 128), F32),
            pltpu.VMEM((SLOTS // 256, 256, 512), BF),
            pltpu.VMEM((ORB * ORB, SLOTS), BF),
            pltpu.SemaphoreType.DMA((len(operands),)),
            pltpu.SemaphoreType.DMA((6,)),
            pltpu.SemaphoreType.DMA((4,)),
            pltpu.SemaphoreType.DMA((4,)),
        ],
        compiler_params=pltpu.CompilerParams(
            collective_id=0, has_side_effects=True, vmem_limit_bytes=60 << 20
        ),
    )(*operands)


def solution(mesh):
    spread = ("gx", "gy", "layer")
    placed = (P(spread, None), P(spread, None)) + (P(spread),) * 6 + (P(),) * 8
    return jax.shard_map(
        shards, mesh=mesh, in_specs=placed, out_specs=P(None, spread), check_vma=False
    )
```

```python
import jax
import jax.numpy as jnp
from jax import lax
from jax.experimental import pallas as pl
from jax.experimental.pallas import tpu as pltpu
from jax.sharding import PartitionSpec as P

ORB = 13
LAYERS = 3
OFFSETS = 18
SELF = 4
ATOMS = 64
NEIGH = 72
SLOTS = ATOMS * NEIGH
CAP = 128
LISTED = 2176
MESH = pl.DeviceIdType.MESH
BF = jnp.bfloat16
F32 = jnp.float32
NT = (((1,), (1,)), ((), ()))


def dot(a, b):
    return jnp.dot(a, b, preferred_element_type=F32)


def dot_nt(a, b):
    return lax.dot_general(a, b, NT, preferred_element_type=F32)


def silu(v):
    half = 0.5 * v
    return half + half * jnp.tanh(half)


def reverse_of(offset):
    return offset // 9 * 9 + 8 - offset % 9


def kernel(
    *refs,
):
    sources, out_ref, held = refs[:16], refs[16], refs[17:33]
    (
        ghost,
        hidden,
        bond_send,
        bond_recv,
        line,
        rows,
        flat,
        pick_far,
        mix,
        tables,
        edge,
        last,
        wide,
        spread,
        place,
        result,
        in_sem,
        out_sem,
        send_sem,
        recv_sem,
    ) = refs[33:]
    (
        atom_ref,
        bond_ref,
        dist_ref,
        nbr_ref,
        kind_ref,
        own_ref,
        send_ref,
        recv_ref,
        wl_ref,
        wr_ref,
        wi_ref,
        wo_ref,
        wm_ref,
        wu_ref,
        gain_ref,
        wb_ref,
    ) = held
    gx, gy, sheet = lax.axis_index("gx"), lax.axis_index("gy"), lax.axis_index("layer")
    n_gx, n_gy = lax.axis_size("gx"), lax.axis_size("gy")

    def partner(offset):
        step_x = offset % 9 // 3 - 1
        step_y = offset % 3 - 1
        return (
            (gx + step_x + n_gx) % n_gx,
            (gy + step_y + n_gy) % n_gy,
            (sheet + offset // 9) % 2,
        )

    others = [0, 2, 6, 8, 9, 11, 15, 17, 3, 5, 12, 14, 1, 7, 10, 16, 13]

    barrier = pltpu.get_barrier_semaphore()
    for o in others:
        pl.semaphore_signal(barrier, inc=1, device_id=partner(o), device_id_type=MESH)
    fetches = [
        pltpu.make_async_copy(source, target, in_sem.at[i])
        for i, (source, target) in enumerate(zip(sources, held))
    ]
    for i in (5, 6, 3, 4, 7, 2, 0, 1, 12, 13, 14, 8, 9, 10, 11, 15):
        fetches[i].start()
    def ghost_copy(layer, o):
        source = atom_ref if layer == 0 else hidden.at[layer - 1]
        return pltpu.make_async_remote_copy(
            src_ref=source,
            dst_ref=ghost.at[layer, reverse_of(o)],
            send_sem=send_sem.at[layer],
            recv_sem=recv_sem.at[layer],
            device_id=partner(o),
            device_id_type=MESH,
        )

    def bond_copy(o):
        return pltpu.make_async_remote_copy(
            src_ref=bond_send.at[o],
            dst_ref=bond_recv.at[reverse_of(o)],
            send_sem=send_sem.at[3],
            recv_sem=recv_sem.at[3],
            device_id=partner(o),
            device_id_type=MESH,
        )

    for i in (5, 6, 3, 4, 7, 2):
        fetches[i].wait()

    sub = lax.broadcasted_iota(jnp.int32, (128, 128), 0)
    lane1 = lax.broadcasted_iota(jnp.int32, (1, 128), 1)
    packed = (nbr_ref[...] | (kind_ref[...] << 11) | ((recv_ref[...] & 127) << 13)).astype(F32)
    flat[0 : SLOTS // 128, :] = packed

    def by_slot(source, k):
        for n in range(ATOMS):
            at, first = n * NEIGH // 128, n * NEIGH % 128
            mine = source[at : at + 1, :]
            if first + NEIGH > 128:
                mine = jnp.where(lane1 >= first, mine, source[at + 1 : at + 2, :])
            line[k, n : n + 1, :] = mine
        moved = jnp.concatenate([line[k], line[k]], axis=0)
        for bit in (1, 2, 4, 8):
            moved = jnp.where((sub * 7 & bit) != 0, pltpu.roll(moved, 8 * bit, 1), moved)
        return moved.T[:NEIGH, :]

    slot = by_slot(flat, 0).astype(jnp.int32)
    nbr, kind, place_in = slot & 2047, (slot >> 11) & 3, slot >> 13
    offset_of = nbr >> 6
    atom_of = ((nbr & 63) + 1).astype(F32)
    scaled = by_slot(dist_ref, 1) / 7.0
    falloff = 1.0 - scaled * scaled
    env = jnp.where(kind > 0, falloff * falloff, 0.0)
    own_key = jnp.where(kind == 1, offset_of, -1)
    far_key = jnp.where(kind == 2, offset_of, -1)
    recv_place = (place_in + 1).astype(F32)

    sub72 = lax.broadcasted_iota(jnp.int32, (NEIGH, 128), 0)
    fetches[0].wait()

    pl.semaphore_wait(barrier, len(others))
    for o in others:
        ghost_copy(0, o).start()
    ghost[0, SELF] = atom_ref[...]

    sub384 = lax.broadcasted_iota(jnp.int32, (384, 128), 0)

    def bond_step(step, carry):
        first = step * 384
        picked = [
            jnp.where(send_ref[k : k + 1, :] - first == sub384, 1.0, 0.0).astype(BF)
            for k in range(LISTED // 128)
        ]
        got = dot(jnp.concatenate(picked, axis=1), bond_ref[:LISTED, :]).astype(BF)
        for i in range(3):
            o = step * 3 + i
            bond_send[o] = got[i * 128 : (i + 1) * 128, :]

            @pl.when(o != SELF)
            def _():
                bond_copy(o).start()

        return carry

    fetches[1].wait()
    lax.fori_loop(0, OFFSETS // 3, bond_step, 0)

    def exchange(k):
        mine = bond_recv if k == 3 else ghost.at[k]
        whole = mine.at[pl.ds(0, len(others))]
        return pltpu.make_async_remote_copy(
            src_ref=whole,
            dst_ref=whole,
            send_sem=send_sem.at[k],
            recv_sem=recv_sem.at[k],
            device_id=partner(0),
            device_id_type=MESH,
        )

    def wait_ghost(layer):
        exchange(layer).wait_recv()

    def update_hidden(layer):
        two = dot(mix[...], ghost[layer].reshape(OFFSETS * ATOMS, 128))
        reached = (two[:ATOMS] + two[ATOMS:]).astype(BF)
        summed = (dot(reached, wm_ref[layer]) * 0.125).astype(BF)
        updated = ghost[layer, SELF].astype(F32) + silu(dot(summed, wu_ref[layer]))
        mean = jnp.mean(updated * updated, axis=-1, keepdims=True)
        fresh = updated * lax.rsqrt(mean + 1e-06) * gain_ref[layer : layer + 1, :]
        hidden[layer] = fresh.astype(BF)
        for o in others:
            ghost_copy(layer + 1, o).start()
        ghost[layer + 1, SELF] = fresh.astype(BF)

    def project(layer):
        both = jnp.concatenate([wr_ref[layer], wl_ref[layer]], axis=1)

        got = dot(ghost[layer].reshape(OFFSETS * ATOMS, 128), both).astype(BF)
        for o in range(OFFSETS):
            tables[o, 0:64, 0:128] = got[o * 64 : (o + 1) * 64, :128]
            tables[o, 64:128, 128:256] = got[o * 64 : (o + 1) * 64, 128:]

    def twice(w):
        none = jnp.zeros_like(w)
        return jnp.concatenate(
            [jnp.concatenate([w, none], axis=1), jnp.concatenate([none, w], axis=1)], axis=0
        )

    averages = twice(jnp.full((128, 128), 1.0 / 128.0, BF))

    def edge_inner(layer):
        return dot(edge[...].reshape(OFFSETS * 128, 256), twice(wi_ref[layer]))

    def edge_layer(layer, final, inner):
        right = tables[SELF, 0:64, 0:128].astype(F32)
        left = tables[SELF, 64:128, 128:256].astype(F32)
        near = jnp.concatenate([left, right], axis=1)
        near = jnp.concatenate([near, near] * OFFSETS, axis=0)
        state = edge[...].reshape(OFFSETS * 128, 256)
        reached = [dot(pick_far[o], tables[o]) for o in range(OFFSETS)]
        gate = silu(inner * (jnp.concatenate(reached, axis=0) * near)).astype(BF)
        renewed = state.astype(F32) + dot(gate, twice(wo_ref[layer]))
        mean = dot((renewed * renewed).astype(BF), averages)
        fresh = renewed * lax.rsqrt(mean + 1e-06)
        if final:
            for o in range(OFFSETS):
                mine = fresh[o * 128 : (o + 1) * 128, :]
                last[o * 256 : o * 256 + 128, :] = mine[:, :128]
                last[o * 256 + 128 : o * 256 + 256, :] = mine[:, 128:]
        else:
            edge[...] = fresh.astype(BF).reshape(OFFSETS, 128, 256)

    send_place = jnp.zeros((NEIGH, 128), F32)
    own_rows = own_ref[...].astype(F32)
    own_atom = jnp.floor((own_rows + 0.5) * (1.0 / NEIGH))
    own_slot = own_rows - own_atom * NEIGH
    own_place = ((send_ref[...] & 127) + 1).astype(F32)
    sub_slot, sub_atom = sub72.astype(F32), (sub & 63).astype(F32)
    for k in range(OFFSETS):
        at_slot = jnp.where(own_slot[k : k + 1, :] == sub_slot, 1.0, 0.0).astype(BF)
        at_atom = jnp.where(own_atom[k : k + 1, :] == sub_atom, own_place[k : k + 1, :], 0.0)
        send_place = send_place + dot_nt(at_slot, at_atom.astype(BF))

    before = jnp.where(
        lax.broadcasted_iota(jnp.int32, (NEIGH, NEIGH), 0)
        > lax.broadcasted_iota(jnp.int32, (NEIGH, NEIGH), 1),
        1.0,
        0.0,
    ).astype(BF)
    rank_lane = (lax.broadcasted_iota(jnp.int32, (NEIGH, 128), 1) >> 6).astype(F32)

    def total(v):
        return jnp.sum(v, axis=0, keepdims=True)

    def tables_step(o, where_to):
        own = jnp.where(own_key == o, 1.0, 0.0)
        far = jnp.where(far_key == o, 1.0, 0.0)
        count = dot(before, jnp.concatenate([own, far], axis=1).astype(BF))
        own_rank, far_rank = count[:, :128], count[:, 128:]
        own_hit = jnp.where(own_rank == rank_lane, own, 0.0)
        far_hit = jnp.where(far_rank == rank_lane, far, 0.0)
        rows[0, pl.ds(o, 1), :] = total(own_hit * atom_of) - 1.0
        rows[1, pl.ds(o, 1), :] = total(far_hit * atom_of) - 1.0
        rows[2, pl.ds(o, 1), :] = total(own_hit * send_place) - 1.0
        rows[3, pl.ds(o, 1), :] = total(far_hit * recv_place) - 1.0
        rows[4, pl.ds(o, 1), :] = total(own_hit * env)
        rows[5, pl.ds(o, 1), :] = total(far_hit * env)
        base = (4 * o + 1).astype(F32)
        return where_to + own * (own_rank + base) + far * (far_rank + (base + 2.0))

    where_to = lax.fori_loop(0, OFFSETS, tables_step, jnp.zeros((NEIGH, 128), F32), unroll=6)

    subf = (sub & 63).astype(F32)
    for g in range(OFFSETS // 2):
        low = sub < 64

        def pair(kind_of_row):
            first = rows[kind_of_row, 2 * g : 2 * g + 1, :]
            second = rows[kind_of_row, 2 * g + 1 : 2 * g + 2, :]
            return jnp.where(low, first, second)

        weights = jnp.where(pair(0) == subf, pair(4), 0.0) + jnp.where(
            pair(1) == subf, pair(5), 0.0
        )
        mix[:, g * 128 : (g + 1) * 128] = weights.T.astype(BF)

    def far_step(o, carry):
        own_atom, far_atom = rows[0, pl.ds(o, 1), :], rows[1, pl.ds(o, 1), :]
        wanted = jnp.where(sub < 64, own_atom, far_atom)
        pick_far[o] = jnp.where(wanted == subf, 1.0, 0.0).astype(BF).T
        return carry

    lax.fori_loop(0, OFFSETS, far_step, 0, unroll=6)
    subq = sub.astype(F32)

    def own_step(o, carry):
        picker = jnp.where(rows[2, pl.ds(o, 1), :] == subq, 1.0, 0.0).astype(BF).T
        edge[o, :, 0:128] = dot(picker, bond_send[o]).astype(BF)
        return carry

    lax.fori_loop(0, OFFSETS, own_step, 0, unroll=6)

    for n in range(ATOMS):
        place_of = jnp.broadcast_to(where_to[:, n : n + 1], (NEIGH, 128))
        spread[n * NEIGH : (n + 1) * NEIGH, :] = jnp.where(
            place_of > 0.0, place_of + (n % 32 * NEIGH - 1.0), -1.0
        )

    def place_step(i, carry):
        start = jnp.clip(i % 9 * 256 - 128, 0, SLOTS // 2 - 512)
        wanted = spread[pl.ds(pl.multiple_of(i * 256, 256), 256), :]
        for k in range(4):
            here = lax.broadcasted_iota(jnp.int32, (256, 128), 1) + (start + k * 128)
            place[i, :, k * 128 : (k + 1) * 128] = jnp.where(
                wanted == here.astype(F32), 1.0, 0.0
            ).astype(BF)
        return carry

    lax.fori_loop(0, SLOTS // 256, place_step, 0, unroll=2)

    tables[...] = jnp.zeros_like(tables)
    for i in (12, 13, 14):
        fetches[i].wait()
    wait_ghost(0)
    update_hidden(0)

    for i in (8, 9, 10, 11, 15):
        fetches[i].wait()
    project(0)
    wait_ghost(1)
    update_hidden(1)

    exchange(3).wait_recv()
    bond_recv[SELF] = bond_send[SELF]

    def recv_step(o, carry):
        picker = jnp.where(rows[3, pl.ds(o, 1), :] == subq, 1.0, 0.0).astype(BF).T
        edge[o, :, 128:256] = dot(picker, bond_recv[o]).astype(BF)
        return carry

    lax.fori_loop(0, OFFSETS, recv_step, 0, unroll=6)
    edge_layer(0, False, edge_inner(0))

    project(1)
    edge_layer(1, False, edge_inner(1))
    inner = edge_inner(2)

    row = lax.broadcasted_iota(jnp.int32, (ORB * ORB, ORB * ORB), 0)
    col = lax.broadcasted_iota(jnp.int32, (ORB * ORB, ORB * ORB), 1)
    coarse = jnp.floor((row.astype(F32) + 0.5) * (1.0 / ORB))
    source = (row.astype(F32) - coarse * ORB) * ORB + coarse
    swap = jnp.where(source == col.astype(F32), 1.0, 0.0).astype(BF)
    block_map = jnp.concatenate([wb_ref[...], dot(swap, wb_ref[...]).astype(BF)], axis=1)

    wait_ghost(2)
    project(2)
    edge_layer(2, True, inner)

    half = SLOTS // 2

    def write(c):
        columns = pl.ds(c * 768, 768)
        return pltpu.make_async_copy(
            result.at[:, columns], out_ref.at[:, columns], out_sem.at[c]
        )

    for h in range(2):
        for m in range(h * 16, h * 16 + 16):
            mine = [last[pl.ds(2 * m + i, NEIGH, stride=ATOMS), :] for i in range(2)]
            wide[m * 144 : m * 144 + 144, :] = jnp.concatenate(mine, axis=0).astype(BF)
    for h in range(2):
        states = []
        for i in range(9):
            start = h * half + min(max(i * 256 - 128, 0), half - 512)
            states.append(dot(place[h * 9 + i], wide[start : start + 512, :]).astype(BF).T)
        for i in range(9):
            at = h * half + i * 256
            kinds = [kind_ref[at // 128 + k : at // 128 + k + 1, :] for k in range(2)]
            kinds = jnp.concatenate(kinds, axis=1)
            stacked = [jnp.where(kinds == k, 1.0, 0.0).astype(BF) * states[i] for k in (1, 2)]
            result[:, at : at + 256] = dot(block_map, jnp.concatenate(stacked, axis=0)).astype(BF)
            if i % 3 == 2:
                write(h * 3 + i // 3).start()

    for c in range(6):
        write(c).wait()
    for k in range(4):
        exchange(k).wait_send()


def shards(
    atom_feats,
    bond_embed,
    pair_dist,
    neighbours,
    slot_kind,
    own_rows,
    send_pos,
    recv_pos,
    w_left,
    w_right,
    w_edge_in,
    w_edge_out,
    w_msg,
    w_upd,
    node_gain,
    w_block,
):
    hbm = pl.BlockSpec(memory_space=pltpu.HBM)
    operands = (
        atom_feats,
        bond_embed,
        pair_dist.reshape(SLOTS // 128, 128),
        neighbours.reshape(SLOTS // 128, 128),
        slot_kind.reshape(SLOTS // 128, 128),
        own_rows.reshape(OFFSETS, 128),
        send_pos.reshape(OFFSETS, 128),
        recv_pos.reshape(SLOTS // 128, 128),
        w_left,
        w_right,
        w_edge_in,
        w_edge_out,
        w_msg,
        w_upd,
        node_gain,
        w_block.T,
    )
    return pl.pallas_call(
        kernel,
        out_shape=jax.ShapeDtypeStruct((ORB * ORB, SLOTS), BF),
        in_specs=[hbm] * len(operands),
        out_specs=hbm,
        scratch_shapes=[pltpu.VMEM(v.shape, v.dtype) for v in operands]
        + [
            pltpu.VMEM((LAYERS, OFFSETS, ATOMS, 128), BF),
            pltpu.VMEM((LAYERS - 1, ATOMS, 128), BF),
            pltpu.VMEM((OFFSETS, CAP, 128), BF),
            pltpu.VMEM((OFFSETS, CAP, 128), BF),
            pltpu.VMEM((2, ATOMS, 128), F32),
            pltpu.VMEM((6, 24, 128), F32),
            pltpu.VMEM((40, 128), F32),
            pltpu.VMEM((OFFSETS, 128, 128), BF),
            pltpu.VMEM((128, OFFSETS * ATOMS), BF),
            pltpu.VMEM((OFFSETS, 128, 256), BF),
            pltpu.VMEM((OFFSETS, 128, 256), BF),
            pltpu.VMEM((SLOTS, 128), F32),
            pltpu.VMEM((SLOTS, 128), BF),
            pltpu.VMEM((SLOTS, 128), F32),
            pltpu.VMEM((SLOTS // 256, 256, 512), BF),
            pltpu.VMEM((ORB * ORB, SLOTS), BF),
            pltpu.SemaphoreType.DMA((len(operands),)),
            pltpu.SemaphoreType.DMA((6,)),
            pltpu.SemaphoreType.DMA((4,)),
            pltpu.SemaphoreType.DMA((4,)),
        ],
        compiler_params=pltpu.CompilerParams(
            collective_id=0, has_side_effects=True, vmem_limit_bytes=60 << 20
        ),
    )(*operands)


def solution(mesh):
    spread = ("gx", "gy", "layer")
    placed = (P(spread, None), P(spread, None)) + (P(spread),) * 6 + (P(),) * 8
    return jax.shard_map(
        shards, mesh=mesh, in_specs=placed, out_specs=P(None, spread), check_vma=False
    )
```
